32 devices in a mesh: queue: 16 (over z, y, x), tp: 2 (over core).
Axes of the slice: x: 2, y: 2, z: 4, core: 2. Of those that a mesh axis runs over, the one named last changes fastest.
Arguments:
- latent: bfloat16 [16, 128, 3072], P('queue', None, 'tp'), may hold values from -6 to 6
- step_index: int32 [16], P('queue'), may hold values from 0 to 49
- back_reach: int32 [16], P('queue'), may hold values from 1 to 2
- ahead_reach: int32 [16], P('queue'), may hold values from 1 to 2
- level_mod: float32 [50, 2, 3072], replicated, may hold values from -20 to 20
- text_mod: float32 [2, 2, 3072], replicated, may hold values from -3 to 3
- w_qkv: bfloat16 [3, 3072, 1536], P(None, None, 'tp'), may hold values from -0.109375 to 0.109375
- w_out: bfloat16 [1536, 3072], P('tp'), may hold values from -0.15625 to 0.15625
- keep_coef: float32 [50], replicated, may hold values from 0.6 to 1
- noise_coef: float32 [50], replicated, may hold values from 0.2 to 1
Outputs:
- rolled: bfloat16 [16, 128, 3072], P('queue', None, 'tp')
The draws below stay inside these ranges and needn't reach their ends.
All inputs are finite; a program needn't handle non-finite values.
Results may differ from the reference program's by a relative error of at most 0.012.
The reference program's roundings to bfloat16 on the way (of `normed`, `probs`, `attended` and `renewed`) count: a program that leaves them out, or rounds other values in their place, can miss the bound.
Values may be sent and summed in bfloat16 or wider, within the bound.
A program may use at most 128 MiB of HBM per device.

```python
import math
import jax
import jax.numpy as jnp
from jax import lax

D = 3072
HEADS = 24
HDIM = 64
S = 128
LEVELS = 50
REACH = 2
FRAMES = 16


def draw_level_mod(key, part):
    key_shift = jax.random.fold_in(key, 11)
    key_scale = jax.random.fold_in(key, 12)
    shift_terms = 0.3 * jax.random.normal(key_shift, (LEVELS, D), jnp.float32)
    scale_terms = 0.3 * jax.random.normal(key_scale, (LEVELS, D), jnp.float32)
    shift_terms = jnp.clip(shift_terms, -20.0, 20.0)
    scale_terms = jnp.clip(scale_terms, -20.0, 20.0)
    return jnp.stack([shift_terms, scale_terms], axis=1)


def touch_ends(result, key, smallest, top_value):
    dims = result.shape
    spot = [jax.random.randint(jax.random.fold_in(key, axis), (), 0, dims[axis]) for axis in range(len(dims))]
    result = result.at[tuple(spot)].set(smallest)
    longest = dims.index(max(dims))
    spot[longest] = (spot[longest] + 1) % dims[longest]
    return result.at[tuple(spot)].set(top_value)


def level_of(stream_key, extent, cuts, smallest, high):
    level = 1.0
    for dim, parts in cuts:
        heights = jax.random.uniform(jax.random.fold_in(jax.random.fold_in(stream_key, 6), dim), (parts,), jnp.float32, smallest / len(cuts), high / len(cuts))
        level = level * jnp.repeat(jnp.exp(heights), extent[dim] // parts).reshape((-1,) + (1,) * (len(extent) - 1 - dim))
    return level


def noise(stream_key, extent, scale, bound, split=(), kind=jnp.bfloat16):
    entries = scale * jax.random.normal(stream_key, extent, jnp.float32)
    if split:
        entries = entries * level_of(stream_key, extent, split, -0.22, 0.18)
    return jnp.clip(entries, -bound, bound).astype(kind)


def setup_inputs(seed: int = 0) -> dict:
    arg_keys = jax.random.split(jax.random.key(seed), 11)
    return {
        "latent": noise(arg_keys[0], (FRAMES, S, D), 1.0, 6.0, ((0, 16), (2, 2))),
        "step_index": touch_ends(jax.random.randint(arg_keys[1], (FRAMES,), 0, LEVELS), jax.random.fold_in(arg_keys[1], 1), 0, LEVELS - 1).astype(jnp.int32),
        "back_reach": touch_ends(jax.random.randint(arg_keys[2], (FRAMES,), 1, REACH + 1), jax.random.fold_in(arg_keys[2], 1), 1, REACH).astype(jnp.int32),
        "ahead_reach": touch_ends(jax.random.randint(arg_keys[3], (FRAMES,), 1, REACH + 1), jax.random.fold_in(arg_keys[3], 1), 1, REACH).astype(jnp.int32),
        "level_mod": draw_level_mod(jax.random.fold_in(arg_keys[10], 71), 0),
        "text_mod": noise(arg_keys[5], (2, 2, D), 0.5, 3.0, (), jnp.float32),
        "w_qkv": noise(arg_keys[6], (3, D, HEADS * HDIM), D ** -0.5, 0.109375, ((2, 2),)),
        "w_out": noise(arg_keys[7], (HEADS * HDIM, D), (HEADS * HDIM) ** -0.5, 0.15625, ((0, 2),)),
        "keep_coef": jnp.clip(jax.random.uniform(arg_keys[8], (LEVELS,), jnp.float32, 0.6, 1.0), 0.6, 1.0),
        "noise_coef": jnp.clip(jnp.exp(jax.random.uniform(arg_keys[9], (LEVELS,), jnp.float32, math.log(0.2), math.log(1.0))), 0.2, 1.0),
    }


epsilon = 1e-06
guidance = 6.0

def reference(latent, step_index, back_reach, ahead_reach, level_mod, text_mod, w_qkv, w_out, keep_coef, noise_coef):
    frames = latent.shape[0]
    tokens = latent.shape[1]
    gathered = latent.astype(jnp.float32)
    row_mean = lax.optimization_barrier(jnp.mean(gathered, axis=-1, keepdims=True))
    centred = gathered - row_mean
    spread = lax.optimization_barrier(jnp.mean(centred * centred, axis=-1, keepdims=True))
    unit_rows = centred * lax.rsqrt(spread + epsilon)
    modulation = level_mod[step_index]
    shift_terms = modulation[:, 0][:, None, :] + text_mod[None, :, 0]
    scale_terms = modulation[:, 1][:, None, :] + text_mod[None, :, 1]
    normed = (unit_rows[:, None] * (1.0 + scale_terms[:, :, None, :]) + shift_terms[:, :, None, :]).astype(jnp.bfloat16)
    flat = normed.reshape(frames * 2 * tokens, D)
    queries = jnp.dot(flat, w_qkv[0], preferred_element_type=jnp.float32).astype(jnp.bfloat16)
    key_rows = jnp.dot(flat, w_qkv[1], preferred_element_type=jnp.float32).astype(jnp.bfloat16)
    value_rows = jnp.dot(flat, w_qkv[2], preferred_element_type=jnp.float32).astype(jnp.bfloat16)
    queries = queries.reshape(frames, 2, tokens, HEADS, HDIM)
    key_rows = key_rows.reshape(frames, 2, tokens, HEADS, HDIM)
    value_rows = value_rows.reshape(frames, 2, tokens, HEADS, HDIM)
    padding = ((REACH, REACH), (0, 0), (0, 0), (0, 0), (0, 0))
    keys_padded = jnp.pad(key_rows, padding)
    values_padded = jnp.pad(value_rows, padding)
    offsets = jnp.arange(-REACH, REACH + 1, dtype=jnp.int32)
    span = 2 * REACH + 1

    def attend(frame_at):
        key_window = lax.dynamic_slice_in_dim(keys_padded, frame_at, span, 0)
        value_window = lax.dynamic_slice_in_dim(values_padded, frame_at, span, 0)
        key_window = jnp.transpose(key_window, (1, 0, 2, 3, 4)).reshape(2, span * tokens, HEADS, HDIM)
        value_window = jnp.transpose(value_window, (1, 0, 2, 3, 4)).reshape(2, span * tokens, HEADS, HDIM)
        back_now = lax.dynamic_index_in_dim(back_reach, frame_at, 0, keepdims=False)
        ahead_now = lax.dynamic_index_in_dim(ahead_reach, frame_at, 0, keepdims=False)
        target = frame_at + offsets
        allowed = (offsets >= -back_now) & (offsets <= ahead_now) & (target >= 0) & (target < frames)
        key_mask = jnp.repeat(allowed, tokens)
        query_now = lax.dynamic_index_in_dim(queries, frame_at, 0, keepdims=False)
        scores = jnp.einsum('bshd,bkhd->bhsk', query_now.astype(jnp.float32), key_window.astype(jnp.float32)) * HDIM ** (-0.5)
        scores = jnp.where(key_mask[None, None, None, :], scores, -1e+30)
        top = lax.optimization_barrier(jnp.max(scores, axis=-1, keepdims=True))
        expon = jnp.exp(scores - top)
        probs = (expon / lax.optimization_barrier(jnp.sum(expon, axis=-1, keepdims=True))).astype(jnp.bfloat16)
        attended = jnp.einsum('bhsk,bkhd->bshd', probs.astype(jnp.float32), value_window.astype(jnp.float32))
        return attended.astype(jnp.bfloat16).reshape(2, tokens, HEADS * HDIM)
    attended = lax.map(attend, jnp.arange(frames, dtype=jnp.int32))
    predicted = jnp.dot(attended.reshape(frames * 2 * tokens, HEADS * HDIM), w_out, preferred_element_type=jnp.float32)
    predicted = predicted.reshape(frames, 2, tokens, D)
    guided = predicted[:, 1] + guidance * (predicted[:, 0] - predicted[:, 1])
    keep_now = keep_coef[step_index][:, None, None]
    noise_now = noise_coef[step_index][:, None, None]
    renewed = (keep_now * gathered - noise_now * guided).astype(jnp.bfloat16)
    return jnp.roll(renewed, 1, axis=0)
```

```python
import functools

import jax
import jax.numpy as jnp
from jax import lax
from jax.experimental import pallas as pl
from jax.experimental.pallas import tpu as pltpu
from jax.sharding import PartitionSpec as P

HDIM = 64
REACH = 2
SPAN = 2 * REACH + 1
epsilon = 1e-06
guidance = 6.0
MESH = pl.DeviceIdType.MESH

CHUNKS = 4
TILE = 256
OUT_TILE = 512
ROWS = 16

OWN, X, Y, Z, R = range(5)


def kernel(
    n,
    step_ref,
    back_ref,
    ahead_ref,
    keep_ref,
    noise_ref,
    level_ref,
    text_ref,
    latent_hbm,
    wqkv_hbm,
    wout_hbm,
    out_ref,
    frames,
    mods,
    wqkv,
    wout,
    nbuf,
    qbuf,
    kbuf,
    vbuf,
    mix,
    give,
    take,
    stage,
    own_sem,
    wq_sem,
    wo_sem,
    mod_send,
    mod_recv,
    par_send,
    par_recv,
    xy_send,
    z_send,
    r_send,
    ici_recv,
    give_send,
    take_recv,
    roll_send,
    roll_recv,
):
    p = lax.axis_index("queue")
    t = lax.axis_index("tp")
    o = 1 - t
    tokens, half = out_ref.shape
    cols = wqkv.shape[2]
    rows_c = tokens // CHUNKS
    low = lax.rem(p, 2)
    mid = lax.rem(p // 2, 2)
    xp = p + 1 - 2 * low
    yp = p + 2 - 4 * mid
    zdir = 1 - 2 * mid
    zto = p + 4 * zdir
    zfrom = p - 4 * zdir
    has_zto = (zto >= 0) & (zto < n)
    has_zfrom = (zfrom >= 0) & (zfrom < n)
    relays_y = low == mid
    relays_z = low != mid
    has_r = relays_z | has_zfrom
    following = lax.rem(p + 1, n)
    preceding = lax.rem(p + n - 1, n)
    offsets = (0, 1 - 2 * low, 2 - 4 * mid, 4 * mid - 2, 2 * low - 1)

    own_copy = pltpu.make_async_copy(latent_hbm.at[0], frames.at[OWN, t], own_sem)
    own_copy.start()
    w_copies = [
        pltpu.make_async_copy(wqkv_hbm.at[i], wqkv.at[i], wq_sem.at[i]) for i in range(3)
    ]
    for i in range(3):
        w_copies[i].start()
    wo_copy = pltpu.make_async_copy(wout_hbm, wout, wo_sem)
    wo_copy.start()
    step = step_ref[0]
    mods[REACH] = level_ref[step]

    barrier = pltpu.get_barrier_semaphore()

    def greet(q, tp):
        pl.semaphore_signal(barrier, inc=1, device_id=(q, tp), device_id_type=MESH)

    greet(p, o)
    greet(xp, t)
    greet(yp, t)
    greet(following, t)
    greet(preceding, t)
    optional = [
        (has_zto, zto),
        (has_zfrom, zfrom),
        (p + 1 < n, p + 1),
        (p >= 1, p - 1),
        (p + 2 < n, p + 2),
        (p >= 2, p - 2),
    ]
    for cond, q in optional:
        @pl.when(cond)
        def _(q=q):
            greet(q, t)
    pl.semaphore_wait(barrier, 5 + sum(cond.astype(jnp.int32) for cond, _ in optional))
    own_copy.wait()

    def remote(src, dst, ssem, rsem, q, tp):
        return pltpu.make_async_remote_copy(
            src_ref=src, dst_ref=dst, send_sem=ssem, recv_sem=rsem,
            device_id=(q, tp), device_id_type=MESH,
        )

    def piece(slot, side, c):
        return frames.at[slot, side, pl.ds(c * rows_c, rows_c)]

    def to_partner(slot, c):
        return remote(piece(slot, t, c), piece(slot, t, c),
                      par_send.at[slot, c], par_recv.at[slot, c], p, o)

    def from_partner(slot, c):
        return remote(piece(slot, o, c), piece(slot, o, c),
                      par_send.at[slot, c], par_recv.at[slot, c], p, o)

    def own_to(slot, c):
        return remote(piece(OWN, t, c), piece(slot, t, c),
                      xy_send.at[slot - X, c], ici_recv.at[slot - X, c],
                      xp if slot == X else yp, t)

    def y_to_z(c):
        return remote(piece(Y, t, c), piece(Z, t, c),
                      z_send.at[c], ici_recv.at[Z - X, c], zto, t)

    def slot_to_r(slot, c):
        return remote(piece(slot, t, c), piece(R, t, c),
                      r_send.at[c], ici_recv.at[R - X, c], xp, t)

    def mod_to(d):
        return remote(mods.at[REACH], mods.at[REACH - d],
                      mod_send.at[REACH + d], mod_recv.at[REACH - d], p + d, t)

    for c in range(CHUNKS):
        own_to(Y, c).start()
        own_to(X, c).start()
        to_partner(OWN, c).start()
    for d in (1, -1, 2, -2):
        @pl.when((p + d >= 0) & (p + d < n))
        def _(d=d):
            mod_to(d).start()

    def arrived(slot, c):
        remote(piece(slot, t, c), piece(slot, t, c), xy_send.at[0, c],
               ici_recv.at[slot - X, c], xp, t).wait_recv()

    def relay_x(c):
        arrived(X, c)
        to_partner(X, c).start()

    def relay_y(c):
        arrived(Y, c)

        @pl.when(has_zto)
        def _():
            y_to_z(c).start()

        @pl.when(relays_y)
        def _():
            slot_to_r(Y, c).start()
        to_partner(Y, c).start()

    def relay_z(c):
        @pl.when(has_zfrom)
        def _():
            arrived(Z, c)

            @pl.when(relays_z)
            def _():
                slot_to_r(Z, c).start()
            to_partner(Z, c).start()

    def relay_r(c):
        @pl.when(has_r)
        def _():
            arrived(R, c)
            to_partner(R, c).start()

    def clear(slot):
        frames[slot] = jnp.zeros(frames.shape[1:], frames.dtype)

    @pl.when(jnp.logical_not(has_zfrom))
    def _():
        clear(Z)

    @pl.when(jnp.logical_not(has_r))
    def _():
        clear(R)

    for d in (1, -1, 2, -2):
        @pl.when((p + d < 0) | (p + d >= n))
        def _(d=d):
            mods[REACH + d] = jnp.zeros(mods.shape[1:], mods.dtype)

    def normalize(slot, base):
        modulation = mods[REACH + offsets[slot]]
        text = text_ref[...]
        shift = [modulation[0:1] + text[b, 0:1] for b in range(2)]
        scale = [1.0 + (modulation[1:2] + text[b, 1:2]) for b in range(2)]

        def body(i, carry):
            at = pl.ds(pl.multiple_of(i * ROWS, ROWS), ROWS)
            parts = [frames[slot, h, at, :].astype(jnp.float32) for h in range(2)]
            total = sum(jnp.sum(v, axis=-1, keepdims=True) for v in parts)
            mean = total * (1.0 / (2 * half))
            parts = [v - mean for v in parts]
            spread = sum(jnp.sum(v * v, axis=-1, keepdims=True) for v in parts)
            inv = lax.rsqrt(spread * (1.0 / (2 * half)) + epsilon)
            for h in range(2):
                span = slice(h * half, (h + 1) * half)
                unit = parts[h] * inv
                for b in range(2):
                    row = pl.ds(pl.multiple_of(base + b * tokens + i * ROWS, ROWS), ROWS)
                    nbuf[row, span] = (
                        unit * scale[b][:, span] + shift[b][:, span]
                    ).astype(nbuf.dtype)
            return carry

        lax.fori_loop(0, tokens // ROWS, body, 0)

    def project(kind, slots):
        m = 2 * tokens * len(slots)

        def body(j, carry):
            at = pl.ds(pl.multiple_of(j * TILE, TILE), TILE)
            res = jnp.dot(
                nbuf[0:m, :], wqkv[kind, :, at], preferred_element_type=jnp.float32
            )
            if kind == 0:
                res = res * HDIM ** (-0.5)
            res = res.astype(jnp.bfloat16)
            for k, slot in enumerate(slots):
                for b in range(2):
                    rows = res[(2 * k + b) * tokens : (2 * k + b + 1) * tokens]
                    if kind == 0:
                        qbuf[b, :, at] = rows
                    else:
                        dst = kbuf if kind == 1 else vbuf
                        dst[b, slot * tokens : (slot + 1) * tokens, at] = rows
            return carry

        lax.fori_loop(0, cols // TILE, body, 0)

    def mod_arrives(d):
        @pl.when((p + d >= 0) & (p + d < n))
        def _():
            remote(mods.at[REACH + d], mods.at[REACH + d], mod_send.at[REACH],
                   mod_recv.at[REACH + d], p, o).wait_recv()

    for c in range(CHUNKS):
        from_partner(OWN, c).wait_recv()
    normalize(OWN, 0)
    w_copies[0].wait()
    project(0, (OWN,))
    relay_y(0)
    relay_x(0)
    w_copies[1].wait()
    project(1, (OWN,))
    relay_y(1)
    relay_x(1)
    w_copies[2].wait()
    project(2, (OWN,))
    for d in (1, -1, 2, -2):
        mod_arrives(d)
    for c in range(2, CHUNKS):
        relay_y(c)
        relay_z(c - 2)
        relay_x(c)
    for c in range(CHUNKS):
        from_partner(X, c).wait_recv()
    normalize(X, 0)
    for c in range(CHUNKS):
        from_partner(Y, c).wait_recv()
    relay_r(0)
    normalize(Y, 2 * tokens)
    relay_z(2)
    project(1, (X, Y))
    relay_z(3)
    relay_r(1)
    project(2, (X, Y))
    relay_r(2)

    def slot_full(slot, cond):
        @pl.when(cond)
        def _():
            for c in range(CHUNKS):
                from_partner(slot, c).wait_recv()

    slot_full(Z, has_zfrom)
    normalize(Z, 0)
    relay_r(3)
    slot_full(R, has_r)
    normalize(R, 2 * tokens)
    project(1, (Z, R))
    project(2, (Z, R))

    lane = lax.broadcasted_iota(jnp.int32, (1, SPAN * tokens), 1) // tokens
    bias = jnp.zeros((1, SPAN * tokens), jnp.float32)
    for slot in range(SPAN):
        off = offsets[slot]
        target = p + off
        ok = (off >= -back_ref[0]) & (off <= ahead_ref[0]) & (target >= 0) & (target < n)
        bias = jnp.where(lane == slot, jnp.where(ok, 0.0, -1e30), bias)
    pair = 2 * HDIM
    first = lax.broadcasted_iota(jnp.int32, (1, pair), 1) < HDIM

    def heads(j, carry):
        at = pl.ds(pl.multiple_of(j * pair, pair), pair)
        outs = []
        for b in range(2):
            q = qbuf[b, :, at]
            zero = jnp.zeros_like(q)
            both = jnp.concatenate([jnp.where(first, q, zero), jnp.where(first, zero, q)], axis=0)
            scores = lax.dot_general(
                both, kbuf[b, :, at], (((1,), (1,)), ((), ())),
                preferred_element_type=jnp.float32,
            ) + bias
            top = jnp.max(scores, axis=-1, keepdims=True)
            expon = jnp.exp(scores - top)
            inv = 1.0 / jnp.sum(expon, axis=-1, keepdims=True)
            probs = (expon * inv).astype(jnp.bfloat16)
            att = jnp.dot(probs, vbuf[b, :, at], preferred_element_type=jnp.float32)
            att = jnp.where(first, att[:tokens], att[tokens:])
            outs.append(att.astype(jnp.bfloat16).astype(jnp.float32))
        mixture = outs[1] + guidance * (outs[0] - outs[1])
        upper = mixture.astype(jnp.bfloat16)
        mix[0:tokens, at] = upper
        mix[tokens : 2 * tokens, at] = (mixture - upper.astype(jnp.float32)).astype(jnp.bfloat16)
        return carry

    lax.fori_loop(0, cols // pair, heads, 0)

    wo_copy.wait()
    tiles = half // OUT_TILE

    def partial(side, j):
        at = pl.ds(pl.multiple_of(side * half + j * OUT_TILE, OUT_TILE), OUT_TILE)
        res = jnp.dot(mix[...], wout[:, at], preferred_element_type=jnp.float32)
        return res[:tokens] + res[tokens:]

    def hand(j):
        return remote(give.at[j], take.at[j], give_send.at[j], take_recv.at[j], p, o)

    def rolled(j):
        return remote(stage.at[j], out_ref.at[:, j * OUT_TILE : (j + 1) * OUT_TILE],
                      roll_send.at[j], roll_recv.at[j], following, t)

    for j in range(tiles):
        give[j] = partial(o, j)
        hand(j).start()
    keep = keep_ref[step]
    noise = noise_ref[step]
    for j in range(tiles):
        mine = partial(t, j)
        hand(j).wait_recv()
        guided = mine + take[j]
        current = frames[OWN, t, :, j * OUT_TILE : (j + 1) * OUT_TILE].astype(jnp.float32)
        stage[j] = (keep * current - noise * guided).astype(stage.dtype)
        rolled(j).start()

    for c in range(CHUNKS):
        own_to(X, c).wait_send()
        own_to(Y, c).wait_send()
        for slot in (OWN, X, Y):
            to_partner(slot, c).wait_send()

        @pl.when(has_zto)
        def _(c=c):
            y_to_z(c).wait_send()

        @pl.when(has_zfrom)
        def _(c=c):
            to_partner(Z, c).wait_send()

        @pl.when(relays_y | has_zfrom)
        def _(c=c):
            slot_to_r(Y, c).wait_send()

        @pl.when(has_r)
        def _(c=c):
            to_partner(R, c).wait_send()
    for d in (1, -1, 2, -2):
        @pl.when((p + d >= 0) & (p + d < n))
        def _(d=d):
            mod_to(d).wait_send()
    for j in range(tiles):
        hand(j).wait_send()
        rolled(j).wait()


def on_device(
    latent, step_index, back_reach, ahead_reach, level_mod, text_mod,
    w_qkv, w_out, keep_coef, noise_coef,
):
    n = lax.axis_size("queue")
    _, tokens, half = latent.shape
    cols = w_qkv.shape[2]
    tiles = half // OUT_TILE
    dma = pltpu.SemaphoreType.DMA
    bf16, f32 = jnp.bfloat16, jnp.float32
    smem = pl.BlockSpec(memory_space=pltpu.SMEM)
    vmem = pl.BlockSpec(memory_space=pltpu.VMEM)
    hbm = pl.BlockSpec(memory_space=pl.ANY)
    out = pl.pallas_call(
        functools.partial(kernel, n),
        out_shape=jax.ShapeDtypeStruct((tokens, half), bf16),
        in_specs=[smem] * 5 + [vmem] * 2 + [hbm] * 3,
        out_specs=vmem,
        scratch_shapes=[
            pltpu.VMEM((SPAN, 2, tokens, half), bf16),
            pltpu.VMEM((SPAN, 2, 2 * half), f32),
            pltpu.VMEM(w_qkv.shape, bf16),
            pltpu.VMEM(w_out.shape, bf16),
            pltpu.VMEM((4 * tokens, 2 * half), bf16),
            pltpu.VMEM((2, tokens, cols), bf16),
            pltpu.VMEM((2, SPAN * tokens, cols), bf16),
            pltpu.VMEM((2, SPAN * tokens, cols), bf16),
            pltpu.VMEM((2 * tokens, cols), bf16),
            pltpu.VMEM((tiles, tokens, OUT_TILE), f32),
            pltpu.VMEM((tiles, tokens, OUT_TILE), f32),
            pltpu.VMEM((tiles, tokens, OUT_TILE), bf16),
            dma, dma((3,)), dma,
            dma((SPAN,)), dma((SPAN,)),
            dma((SPAN, CHUNKS)), dma((SPAN, CHUNKS)),
            dma((2, CHUNKS)), dma((CHUNKS,)), dma((CHUNKS,)), dma((4, CHUNKS)),
            dma((tiles,)), dma((tiles,)), dma((tiles,)), dma((tiles,)),
        ],
        compiler_params=pltpu.CompilerParams(
            collective_id=0, has_side_effects=True, vmem_limit_bytes=62 * 1024 * 1024
        ),
    )(
        step_index, back_reach, ahead_reach, keep_coef, noise_coef, level_mod, text_mod,
        latent, w_qkv, w_out,
    )
    return out[None]


def solution(mesh):
    return jax.shard_map(
        on_device,
        mesh=mesh,
        in_specs=(
            P("queue", None, "tp"),
            P("queue"),
            P("queue"),
            P("queue"),
            P(),
            P(),
            P(None, None, "tp"),
            P("tp", None),
            P(),
            P(),
        ),
        out_specs=P("queue", None, "tp"),
        check_vma=False,
    )
```

```python
import functools

import jax
import jax.numpy as jnp
from jax import lax
from jax.experimental import pallas as pl
from jax.experimental.pallas import tpu as pltpu
from jax.sharding import PartitionSpec as P

HDIM = 64
REACH = 2
SPAN = 2 * REACH + 1
epsilon = 1e-06
guidance = 6.0
MESH = pl.DeviceIdType.MESH

CHUNKS = 4
TILE = 256
OUT_TILE = 512
ROWS = 16

OWN, X, Y, Z, R = range(5)


def kernel(
    n,
    step_ref,
    back_ref,
    ahead_ref,
    keep_ref,
    noise_ref,
    level_ref,
    text_ref,
    latent_hbm,
    wqkv_hbm,
    wout_hbm,
    out_ref,
    frames,
    mods,
    wqkv,
    wout,
    nbuf,
    qbuf,
    kbuf,
    vbuf,
    mix,
    give,
    take,
    mix_out,
    coefs,
    own_sem,
    wq_sem,
    wo_sem,
    mod_send,
    mod_recv,
    par_send,
    par_recv,
    xy_send,
    z_send,
    r_send,
    ici_recv,
    give_send,
    take_recv,
    roll_send,
    roll_recv,
    coef_send,
    coef_recv,
    wrap_send,
    wrap_recv,
):
    p = lax.axis_index("queue")
    t = lax.axis_index("tp")
    o = 1 - t
    tokens, half = out_ref.shape
    cols = wqkv.shape[2]
    rows_c = tokens // CHUNKS
    low = lax.rem(p, 2)
    mid = lax.rem(p // 2, 2)
    xp = p + 1 - 2 * low
    yp = p + 2 - 4 * mid
    zdir = 1 - 2 * mid
    zto = p + 4 * zdir
    zfrom = p - 4 * zdir
    has_zto = (zto >= 0) & (zto < n)
    has_zfrom = (zfrom >= 0) & (zfrom < n)
    relays_y = low == mid
    relays_z = low != mid
    has_r = relays_z | has_zfrom
    following = lax.rem(p + 1, n)
    preceding = lax.rem(p + n - 1, n)
    offsets = (0, 1 - 2 * low, 2 - 4 * mid, 4 * mid - 2, 2 * low - 1)

    own_copy = pltpu.make_async_copy(latent_hbm.at[0], frames.at[OWN, t], own_sem)
    own_copy.start()
    w_copies = [
        pltpu.make_async_copy(wqkv_hbm.at[i], wqkv.at[i], wq_sem.at[i]) for i in range(3)
    ]
    for i in range(3):
        w_copies[i].start()
    wo_copy = pltpu.make_async_copy(wout_hbm, wout, wo_sem)
    wo_copy.start()
    step = step_ref[0]
    mods[REACH] = level_ref[step]
    coefs[0, 0] = jnp.full(coefs.shape[2:], keep_ref[step], jnp.float32)
    coefs[0, 1] = jnp.full(coefs.shape[2:], noise_ref[step], jnp.float32)

    def clear(slot):
        frames[slot] = jnp.zeros(frames.shape[1:], frames.dtype)

    @pl.when(jnp.logical_not(has_zfrom))
    def _():
        clear(Z)

    @pl.when(jnp.logical_not(has_r))
    def _():
        clear(R)

    for d in (1, -1, 2, -2):
        @pl.when((p + d < 0) | (p + d >= n))
        def _(d=d):
            mods[REACH + d] = jnp.zeros(mods.shape[1:], mods.dtype)

    barrier = pltpu.get_barrier_semaphore()

    def greet(q, tp):
        pl.semaphore_signal(barrier, inc=1, device_id=(q, tp), device_id_type=MESH)

    greet(p, o)
    greet(xp, t)
    greet(yp, t)
    greet(following, t)
    greet(preceding, t)
    optional = [
        (has_zto, zto),
        (has_zfrom, zfrom),
        (p + 1 < n, p + 1),
        (p >= 1, p - 1),
        (p + 2 < n, p + 2),
        (p >= 2, p - 2),
    ]
    for cond, q in optional:
        @pl.when(cond)
        def _(q=q):
            greet(q, t)
    pl.semaphore_wait(barrier, 5 + sum(cond.astype(jnp.int32) for cond, _ in optional))
    own_copy.wait()

    def remote(src, dst, ssem, rsem, q, tp):
        return pltpu.make_async_remote_copy(
            src_ref=src, dst_ref=dst, send_sem=ssem, recv_sem=rsem,
            device_id=(q, tp), device_id_type=MESH,
        )

    def piece(slot, side, c):
        return frames.at[slot, side, pl.ds(c * rows_c, rows_c)]

    def to_partner(slot, c):
        return remote(piece(slot, t, c), piece(slot, t, c),
                      par_send.at[slot, c], par_recv.at[slot, c], p, o)

    def from_partner(slot, c):
        return remote(piece(slot, o, c), piece(slot, o, c),
                      par_send.at[slot, c], par_recv.at[slot, c], p, o)

    def own_to(slot, c):
        return remote(piece(OWN, t, c), piece(slot, t, c),
                      xy_send.at[slot - X, c], ici_recv.at[slot - X, c],
                      xp if slot == X else yp, t)

    def y_to_z(c):
        return remote(piece(Y, t, c), piece(Z, t, c),
                      z_send.at[c], ici_recv.at[Z - X, c], zto, t)

    def slot_to_r(slot, c):
        return remote(piece(slot, t, c), piece(R, t, c),
                      r_send.at[c], ici_recv.at[R - X, c], xp, t)

    def mod_to(d):
        return remote(mods.at[REACH], mods.at[REACH - d],
                      mod_send.at[REACH + d], mod_recv.at[REACH - d], p + d, t)

    for c in range(CHUNKS):
        own_to(Y, c).start()
        own_to(X, c).start()
        to_partner(OWN, c).start()
    for d in (1, -1, 2, -2):
        @pl.when((p + d >= 0) & (p + d < n))
        def _(d=d):
            mod_to(d).start()
    coef_copy = remote(coefs.at[0], coefs.at[1], coef_send, coef_recv, following, t)
    coef_copy.start()

    wrap_copy = remote(frames.at[OWN, t], frames.at[R, t], wrap_send, wrap_recv, following, t)

    @pl.when(p == n - 1)
    def _():
        wrap_copy.start()

    def arrived(slot, c):
        remote(piece(slot, t, c), piece(slot, t, c), xy_send.at[0, c],
               ici_recv.at[slot - X, c], xp, t).wait_recv()

    def relay_x(c):
        arrived(X, c)
        to_partner(X, c).start()

    def relay_y(c):
        arrived(Y, c)

        @pl.when(has_zto)
        def _():
            y_to_z(c).start()

        @pl.when(relays_y)
        def _():
            slot_to_r(Y, c).start()
        to_partner(Y, c).start()

    def relay_z(c):
        @pl.when(has_zfrom)
        def _():
            arrived(Z, c)

            @pl.when(relays_z)
            def _():
                slot_to_r(Z, c).start()
            to_partner(Z, c).start()

    def relay_r(c):
        @pl.when(has_r)
        def _():
            arrived(R, c)
            to_partner(R, c).start()

    def normalize(slot, base):
        modulation = mods[REACH + offsets[slot]]
        text = text_ref[...]
        shift = [modulation[0:1] + text[b, 0:1] for b in range(2)]
        scale = [1.0 + (modulation[1:2] + text[b, 1:2]) for b in range(2)]

        def body(i, carry):
            at = pl.ds(pl.multiple_of(i * ROWS, ROWS), ROWS)
            parts = [frames[slot, h, at, :].astype(jnp.float32) for h in range(2)]
            total = sum(jnp.sum(v, axis=-1, keepdims=True) for v in parts)
            mean = total * (1.0 / (2 * half))
            parts = [v - mean for v in parts]
            spread = sum(jnp.sum(v * v, axis=-1, keepdims=True) for v in parts)
            inv = lax.rsqrt(spread * (1.0 / (2 * half)) + epsilon)
            for h in range(2):
                span = slice(h * half, (h + 1) * half)
                unit = parts[h] * inv
                for b in range(2):
                    row = pl.ds(pl.multiple_of(base + b * tokens + i * ROWS, ROWS), ROWS)
                    nbuf[row, span] = (
                        unit * scale[b][:, span] + shift[b][:, span]
                    ).astype(nbuf.dtype)
            return carry

        lax.fori_loop(0, tokens // ROWS, body, 0, unroll=2)

    def project(kind, slots):
        m = 2 * tokens * len(slots)

        def body(j, carry):
            at = pl.ds(pl.multiple_of(j * TILE, TILE), TILE)
            res = jnp.dot(
                nbuf[0:m, :], wqkv[kind, :, at], preferred_element_type=jnp.float32
            )
            if kind == 0:
                res = res * HDIM ** (-0.5)
            res = res.astype(jnp.bfloat16)
            for k, slot in enumerate(slots):
                for b in range(2):
                    rows = res[(2 * k + b) * tokens : (2 * k + b + 1) * tokens]
                    if kind == 0:
                        qbuf[b, :, at] = rows
                    else:
                        dst = kbuf if kind == 1 else vbuf
                        dst[b, slot * tokens : (slot + 1) * tokens, at] = rows
            return carry

        lax.fori_loop(0, cols // TILE, body, 0)

    def mod_arrives(d):
        @pl.when((p + d >= 0) & (p + d < n))
        def _():
            remote(mods.at[REACH + d], mods.at[REACH + d], mod_send.at[REACH],
                   mod_recv.at[REACH + d], p, o).wait_recv()

    for c in range(CHUNKS):
        from_partner(OWN, c).wait_recv()
    normalize(OWN, 0)
    w_copies[0].wait()
    project(0, (OWN,))
    relay_y(0)
    relay_x(0)
    w_copies[1].wait()
    project(1, (OWN,))
    relay_y(1)
    relay_x(1)
    w_copies[2].wait()
    project(2, (OWN,))
    for d in (1, -1, 2, -2):
        mod_arrives(d)
    for c in range(2, CHUNKS):
        relay_y(c)
        relay_z(c - 2)
        relay_x(c)
    for c in range(CHUNKS):
        from_partner(X, c).wait_recv()
    normalize(X, 0)
    for c in range(CHUNKS):
        from_partner(Y, c).wait_recv()
    relay_r(0)
    normalize(Y, 2 * tokens)
    relay_z(2)
    project(1, (X, Y))
    relay_z(3)
    relay_r(1)
    project(2, (X, Y))
    relay_r(2)

    def slot_full(slot, cond):
        @pl.when(cond)
        def _():
            for c in range(CHUNKS):
                from_partner(slot, c).wait_recv()

    slot_full(Z, has_zfrom)
    normalize(Z, 0)
    relay_r(3)
    slot_full(R, has_r)

    @pl.when(p == 0)
    def _():
        wrap_copy.wait_recv()
    normalize(R, 2 * tokens)
    project(1, (Z, R))
    project(2, (Z, R))

    lane = lax.broadcasted_iota(jnp.int32, (1, SPAN * tokens), 1) // tokens
    bias = jnp.zeros((1, SPAN * tokens), jnp.float32)
    for slot in range(SPAN):
        off = offsets[slot]
        target = p + off
        ok = (off >= -back_ref[0]) & (off <= ahead_ref[0]) & (target >= 0) & (target < n)
        bias = jnp.where(lane == slot, jnp.where(ok, 0.0, -1e30), bias)
    pair = 2 * HDIM
    first = lax.broadcasted_iota(jnp.int32, (1, pair), 1) < HDIM

    def rolled(j):
        at = pl.ds(pl.multiple_of(j * pair, pair), pair)
        return remote(mix_out.at[j], mix.at[:, at], roll_send.at[j], roll_recv.at[j], following, t)

    def heads(j, carry):
        at = pl.ds(pl.multiple_of(j * pair, pair), pair)
        outs = []
        for b in range(2):
            q = qbuf[b, :, at]
            zero = jnp.zeros_like(q)
            both = jnp.concatenate([jnp.where(first, q, zero), jnp.where(first, zero, q)], axis=0)
            scores = lax.dot_general(
                both, kbuf[b, :, at], (((1,), (1,)), ((), ())),
                preferred_element_type=jnp.float32,
            ) + bias
            top = jnp.max(scores, axis=-1, keepdims=True)
            expon = jnp.exp(scores - top)
            inv = 1.0 / jnp.sum(expon, axis=-1, keepdims=True)
            probs = (expon * inv).astype(jnp.bfloat16)
            att = jnp.dot(probs, vbuf[b, :, at], preferred_element_type=jnp.float32)
            att = jnp.where(first, att[:tokens], att[tokens:])
            outs.append(att.astype(jnp.bfloat16).astype(jnp.float32))
        mixture = outs[1] + guidance * (outs[0] - outs[1])
        upper = mixture.astype(jnp.bfloat16)
        mix_out[j, 0:tokens] = upper
        mix_out[j, tokens : 2 * tokens] = (mixture - upper.astype(jnp.float32)).astype(jnp.bfloat16)
        rolled(j).start()
        return carry

    lax.fori_loop(0, cols // pair, heads, 0)

    wo_copy.wait()
    tiles = half // OUT_TILE

    def partial(side, j):
        at = pl.ds(pl.multiple_of(side * half + j * OUT_TILE, OUT_TILE), OUT_TILE)
        res = jnp.dot(mix[...], wout[:, at], preferred_element_type=jnp.float32)
        return res[:tokens] + res[tokens:]

    def hand(j):
        return remote(give.at[j], take.at[j], give_send.at[j], take_recv.at[j], p, o)

    for j in range(cols // pair):
        rolled(j).wait_recv()
    coef_copy.wait_recv()
    for j in range(tiles):
        give[j] = partial(o, j)
        hand(j).start()
    keep = coefs[1, 0, 0:1, 0:1]
    noise = coefs[1, 1, 0:1, 0:1]
    before = low * X + (1 - low) * R
    for j in range(tiles):
        at = slice(j * OUT_TILE, (j + 1) * OUT_TILE)
        mine = partial(t, j)
        hand(j).wait_recv()
        guided = mine + take[j]
        current = frames[before, t, :, at].astype(jnp.float32)
        out_ref[:, at] = (keep * current - noise * guided).astype(out_ref.dtype)

    for c in range(CHUNKS):
        own_to(X, c).wait_send()
        own_to(Y, c).wait_send()
        for slot in (OWN, X, Y):
            to_partner(slot, c).wait_send()

        @pl.when(has_zto)
        def _(c=c):
            y_to_z(c).wait_send()

        @pl.when(has_zfrom)
        def _(c=c):
            to_partner(Z, c).wait_send()

        @pl.when(relays_y | has_zfrom)
        def _(c=c):
            slot_to_r(Y, c).wait_send()

        @pl.when(has_r)
        def _(c=c):
            to_partner(R, c).wait_send()
    for d in (1, -1, 2, -2):
        @pl.when((p + d >= 0) & (p + d < n))
        def _(d=d):
            mod_to(d).wait_send()
    for j in range(tiles):
        hand(j).wait_send()
    for j in range(cols // pair):
        rolled(j).wait_send()
    coef_copy.wait_send()

    @pl.when(p == n - 1)
    def _():
        wrap_copy.wait_send()


def on_device(
    latent, step_index, back_reach, ahead_reach, level_mod, text_mod,
    w_qkv, w_out, keep_coef, noise_coef,
):
    n = lax.axis_size("queue")
    _, tokens, half = latent.shape
    cols = w_qkv.shape[2]
    tiles = half // OUT_TILE
    pairs = cols // (2 * HDIM)
    dma = pltpu.SemaphoreType.DMA
    bf16, f32 = jnp.bfloat16, jnp.float32
    smem = pl.BlockSpec(memory_space=pltpu.SMEM)
    vmem = pl.BlockSpec(memory_space=pltpu.VMEM)
    hbm = pl.BlockSpec(memory_space=pl.ANY)
    out = pl.pallas_call(
        functools.partial(kernel, n),
        out_shape=jax.ShapeDtypeStruct((tokens, half), bf16),
        in_specs=[smem] * 5 + [vmem] * 2 + [hbm] * 3,
        out_specs=vmem,
        scratch_shapes=[
            pltpu.VMEM((SPAN, 2, tokens, half), bf16),
            pltpu.VMEM((SPAN, 2, 2 * half), f32),
            pltpu.VMEM(w_qkv.shape, bf16),
            pltpu.VMEM(w_out.shape, bf16),
            pltpu.VMEM((4 * tokens, 2 * half), bf16),
            pltpu.VMEM((2, tokens, cols), bf16),
            pltpu.VMEM((2, SPAN * tokens, cols), bf16),
            pltpu.VMEM((2, SPAN * tokens, cols), bf16),
            pltpu.VMEM((2 * tokens, cols), bf16),
            pltpu.VMEM((tiles, tokens, OUT_TILE), f32),
            pltpu.VMEM((tiles, tokens, OUT_TILE), f32),
            pltpu.VMEM((pairs, 2 * tokens, 2 * HDIM), bf16),
            pltpu.VMEM((2, 2, 8, 128), f32),
            dma, dma((3,)), dma,
            dma((SPAN,)), dma((SPAN,)),
            dma((SPAN, CHUNKS)), dma((SPAN, CHUNKS)),
            dma((2, CHUNKS)), dma((CHUNKS,)), dma((CHUNKS,)), dma((4, CHUNKS)),
            dma((tiles,)), dma((tiles,)), dma((pairs,)), dma((pairs,)),
            dma, dma, dma, dma,
        ],
        compiler_params=pltpu.CompilerParams(
            collective_id=0, has_side_effects=True, vmem_limit_bytes=62 * 1024 * 1024
        ),
    )(
        step_index, back_reach, ahead_reach, keep_coef, noise_coef, level_mod, text_mod,
        latent, w_qkv, w_out,
    )
    return out[None]


def solution(mesh):
    return jax.shard_map(
        on_device,
        mesh=mesh,
        in_specs=(
            P("queue", None, "tp"),
            P("queue"),
            P("queue"),
            P("queue"),
            P(),
            P(),
            P(None, None, "tp"),
            P("tp", None),
            P(),
            P(),
        ),
        out_specs=P("queue", None, "tp"),
        check_vma=False,
    )
```

```python
import functools

import jax
import jax.numpy as jnp
from jax import lax
from jax.experimental import pallas as pl
from jax.experimental.pallas import tpu as pltpu
from jax.sharding import PartitionSpec as P

HDIM = 64
REACH = 2
SPAN = 2 * REACH + 1
epsilon = 1e-06
guidance = 6.0
MESH = pl.DeviceIdType.MESH

CHUNKS = 4
SPLIT = CHUNKS // 2
TILE = 256
OUT_TILE = 512
ROWS = 16

OWN, X, Y, Z, R = range(5)


def kernel(
    n,
    step_ref,
    back_ref,
    ahead_ref,
    keep_ref,
    noise_ref,
    level_ref,
    text_ref,
    latent_hbm,
    wqkv_hbm,
    wout_hbm,
    out_ref,
    frames,
    mods,
    wqkv,
    wout,
    nbuf,
    qbuf,
    kbuf,
    vbuf,
    mix,
    give,
    take,
    mix_out,
    coefs,
    far,
    own_sem,
    wq_sem,
    wo_sem,
    mod_send,
    mod_recv,
    par_send,
    par_recv,
    xy_send,
    z_send,
    r_send,
    ici_recv,
    give_send,
    take_recv,
    roll_send,
    roll_recv,
    coef_send,
    coef_recv,
    wrap_send,
    wrap_recv,
    far_send,
    far_recv,
):
    p = lax.axis_index("queue")
    t = lax.axis_index("tp")
    o = 1 - t
    tokens, half = out_ref.shape
    cols = wqkv.shape[2]
    rows_c = tokens // CHUNKS
    low = lax.rem(p, 2)
    mid = lax.rem(p // 2, 2)
    xp = p + 1 - 2 * low
    yp = p + 2 - 4 * mid
    zdir = 1 - 2 * mid
    zto = p + 4 * zdir
    zfrom = p - 4 * zdir
    has_zto = (zto >= 0) & (zto < n)
    has_zfrom = (zfrom >= 0) & (zfrom < n)
    relays_y = low == mid
    relays_z = low != mid
    has_r = relays_z | has_zfrom
    following = lax.rem(p + 1, n)
    preceding = lax.rem(p + n - 1, n)
    offsets = (0, 1 - 2 * low, 2 - 4 * mid, 4 * mid - 2, 2 * low - 1)

    own_copy = pltpu.make_async_copy(latent_hbm.at[0], frames.at[OWN, t], own_sem)
    own_copy.start()
    w_copies = [
        pltpu.make_async_copy(wqkv_hbm.at[i], wqkv.at[i], wq_sem.at[i]) for i in range(3)
    ]
    for i in range(3):
        w_copies[i].start()
    wo_copy = pltpu.make_async_copy(wout_hbm, wout, wo_sem)
    wo_copy.start()
    step = step_ref[0]
    mods[REACH] = level_ref[step]
    coefs[0, 0] = jnp.full(coefs.shape[2:], keep_ref[step], jnp.float32)
    coefs[0, 1] = jnp.full(coefs.shape[2:], noise_ref[step], jnp.float32)

    def clear(slot):
        frames[slot] = jnp.zeros(frames.shape[1:], frames.dtype)

    @pl.when(jnp.logical_not(has_zfrom))
    def _():
        clear(Z)

    @pl.when(jnp.logical_not(has_r))
    def _():
        clear(R)

    for d in (1, -1, 2, -2):
        @pl.when((p + d < 0) | (p + d >= n))
        def _(d=d):
            mods[REACH + d] = jnp.zeros(mods.shape[1:], mods.dtype)

    barrier = pltpu.get_barrier_semaphore()

    def greet(q, tp):
        pl.semaphore_signal(barrier, inc=1, device_id=(q, tp), device_id_type=MESH)

    greet(p, o)
    greet(xp, t)
    greet(yp, t)
    greet(following, t)
    greet(preceding, t)
    optional = [
        (has_zto, zto),
        (has_zfrom, zfrom),
        (p + 1 < n, p + 1),
        (p >= 1, p - 1),
        (p + 2 < n, p + 2),
        (p >= 2, p - 2),
    ]
    for cond, q in optional:
        @pl.when(cond)
        def _(q=q):
            greet(q, t)
    pl.semaphore_wait(barrier, 5 + sum(cond.astype(jnp.int32) for cond, _ in optional))
    own_copy.wait()

    def remote(src, dst, ssem, rsem, q, tp):
        return pltpu.make_async_remote_copy(
            src_ref=src, dst_ref=dst, send_sem=ssem, recv_sem=rsem,
            device_id=(q, tp), device_id_type=MESH,
        )

    def piece(slot, side, c):
        return frames.at[slot, side, pl.ds(c * rows_c, rows_c)]

    def to_partner(slot, c):
        return remote(piece(slot, t, c), piece(slot, t, c),
                      par_send.at[slot, c], par_recv.at[slot, c], p, o)

    def from_partner(slot, c):
        return remote(piece(slot, o, c), piece(slot, o, c),
                      par_send.at[slot, c], par_recv.at[slot, c], p, o)

    def own_to(slot, c):
        return remote(piece(OWN, t, c), piece(slot, t, c),
                      xy_send.at[slot - X, c], ici_recv.at[slot - X, c],
                      xp if slot == X else yp, t)

    def y_to_z(c):
        return remote(piece(Y, t, c), piece(Z, t, c),
                      z_send.at[c], ici_recv.at[Z - X, c], zto, t)

    def slot_to_r(slot, c):
        return remote(piece(slot, t, c), piece(R, t, c),
                      r_send.at[c], ici_recv.at[R - X, c], xp if c < SPLIT else yp, t)

    def far_piece(c):
        return far.at[pl.ds((c - SPLIT) * rows_c, rows_c)]

    def x_to_far(c):
        return remote(piece(X, t, c), far_piece(c),
                      far_send.at[c - SPLIT], far_recv.at[c - SPLIT], zfrom, t)

    def far_to_r(c):
        return remote(far_piece(c), piece(R, t, c),
                      r_send.at[c], ici_recv.at[R - X, c], yp, t)

    def mod_to(d):
        return remote(mods.at[REACH], mods.at[REACH - d],
                      mod_send.at[REACH + d], mod_recv.at[REACH - d], p + d, t)

    for c in range(CHUNKS):
        own_to(Y, c).start()
        own_to(X, (c + SPLIT) % CHUNKS).start()
        to_partner(OWN, c).start()
    for d in (1, -1, 2, -2):
        @pl.when((p + d >= 0) & (p + d < n))
        def _(d=d):
            mod_to(d).start()
    coef_copy = remote(coefs.at[0], coefs.at[1], coef_send, coef_recv, following, t)
    coef_copy.start()

    wrap_copy = remote(frames.at[OWN, t], frames.at[R, t], wrap_send, wrap_recv, following, t)

    @pl.when(p == n - 1)
    def _():
        wrap_copy.start()

    def arrived(slot, c):
        remote(piece(slot, t, c), piece(slot, t, c), xy_send.at[0, c],
               ici_recv.at[slot - X, c], xp, t).wait_recv()

    def relay_x(c):
        arrived(X, c)
        if c >= SPLIT:
            @pl.when(relays_y)
            def _():
                slot_to_r(X, c).start()

            @pl.when(relays_z & has_zfrom)
            def _():
                x_to_far(c).start()
        to_partner(X, c).start()

    def relay_far(c):
        @pl.when(relays_z & has_zto)
        def _():
            remote(far_piece(c), far_piece(c), far_send.at[c - SPLIT],
                   far_recv.at[c - SPLIT], xp, t).wait_recv()
            far_to_r(c).start()

    def relay_y(c):
        arrived(Y, c)

        @pl.when(has_zto)
        def _():
            y_to_z(c).start()

        if c < SPLIT:
            @pl.when(relays_y)
            def _():
                slot_to_r(Y, c).start()
        to_partner(Y, c).start()

    def relay_z(c):
        @pl.when(has_zfrom)
        def _():
            arrived(Z, c)

            if c < SPLIT:
                @pl.when(relays_z)
                def _():
                    slot_to_r(Z, c).start()
            to_partner(Z, c).start()

    def relay_r(c):
        @pl.when(has_r)
        def _():
            arrived(R, c)
            to_partner(R, c).start()

    def normalize(slot, base, start=0, stop=CHUNKS):
        modulation = mods[REACH + offsets[slot]]
        text = text_ref[...]
        shift = [modulation[0:1] + text[b, 0:1] for b in range(2)]
        scale = [1.0 + (modulation[1:2] + text[b, 1:2]) for b in range(2)]

        def body(i, carry):
            at = pl.ds(pl.multiple_of(i * ROWS, ROWS), ROWS)
            parts = [frames[slot, h, at, :].astype(jnp.float32) for h in range(2)]
            total = sum(jnp.sum(v, axis=-1, keepdims=True) for v in parts)
            mean = total * (1.0 / (2 * half))
            parts = [v - mean for v in parts]
            spread = sum(jnp.sum(v * v, axis=-1, keepdims=True) for v in parts)
            inv = lax.rsqrt(spread * (1.0 / (2 * half)) + epsilon)
            for h in range(2):
                span = slice(h * half, (h + 1) * half)
                unit = parts[h] * inv
                for b in range(2):
                    row = pl.ds(pl.multiple_of(base + b * tokens + i * ROWS, ROWS), ROWS)
                    nbuf[row, span] = (
                        unit * scale[b][:, span] + shift[b][:, span]
                    ).astype(nbuf.dtype)
            return carry

        lax.fori_loop(start * rows_c // ROWS, stop * rows_c // ROWS, body, 0, unroll=4)

    def project(kind, slots):
        m = 2 * tokens * len(slots)

        def body(j, carry):
            at = pl.ds(pl.multiple_of(j * TILE, TILE), TILE)
            res = jnp.dot(
                nbuf[0:m, :], wqkv[kind, :, at], preferred_element_type=jnp.float32
            )
            if kind == 0:
                res = res * HDIM ** (-0.5)
            res = res.astype(jnp.bfloat16)
            for k, slot in enumerate(slots):
                for b in range(2):
                    rows = res[(2 * k + b) * tokens : (2 * k + b + 1) * tokens]
                    if kind == 0:
                        qbuf[b, :, at] = rows
                    else:
                        dst = kbuf if kind == 1 else vbuf
                        dst[b, slot * tokens : (slot + 1) * tokens, at] = rows
            return carry

        lax.fori_loop(0, cols // TILE, body, 0)

    def mod_arrives(d):
        @pl.when((p + d >= 0) & (p + d < n))
        def _():
            remote(mods.at[REACH + d], mods.at[REACH + d], mod_send.at[REACH],
                   mod_recv.at[REACH + d], p, o).wait_recv()

    def full(slot, chunks, cond=None):
        def waits():
            for c in chunks:
                from_partner(slot, c).wait_recv()
        if cond is None:
            waits()
        else:
            pl.when(cond)(waits)

    full(OWN, range(CHUNKS))
    normalize(OWN, 0)
    relay_y(0)
    relay_x(2)
    w_copies[0].wait()
    project(0, (OWN,))
    w_copies[1].wait()
    project(1, (OWN,))
    relay_y(1)
    relay_x(3)
    w_copies[2].wait()
    project(2, (OWN,))
    relay_far(2)
    relay_z(0)
    for d in (1, -1, 2, -2):
        mod_arrives(d)
    full(X, (2, 3))
    normalize(X, 0, 2, 4)
    relay_y(2)
    relay_x(0)
    relay_far(3)
    relay_z(1)
    full(Y, (0, 1))
    normalize(Y, 2 * tokens, 0, 2)
    relay_r(0)
    relay_r(2)
    relay_y(3)
    relay_x(1)
    full(X, (0, 1))
    normalize(X, 0, 0, 2)
    relay_z(2)
    full(Y, (2, 3))
    normalize(Y, 2 * tokens, 2, 4)
    relay_z(3)
    project(1, (X, Y))
    relay_r(1)
    relay_r(3)
    project(2, (X, Y))
    full(Z, range(CHUNKS), has_zfrom)
    normalize(Z, 0)
    full(R, range(CHUNKS), has_r)

    @pl.when(p == 0)
    def _():
        wrap_copy.wait_recv()
    normalize(R, 2 * tokens)
    project(1, (Z, R))
    project(2, (Z, R))

    lane = lax.broadcasted_iota(jnp.int32, (1, SPAN * tokens), 1) // tokens
    bias = jnp.zeros((1, SPAN * tokens), jnp.float32)
    for slot in range(SPAN):
        off = offsets[slot]
        target = p + off
        ok = (off >= -back_ref[0]) & (off <= ahead_ref[0]) & (target >= 0) & (target < n)
        bias = jnp.where(lane == slot, jnp.where(ok, 0.0, -1e30), bias)
    pair = 2 * HDIM
    first = lax.broadcasted_iota(jnp.int32, (1, pair), 1) < HDIM

    def rolled(j):
        at = pl.ds(pl.multiple_of(j * pair, pair), pair)
        return remote(mix_out.at[j], mix.at[:, at], roll_send.at[j], roll_recv.at[j], following, t)

    def heads(j, carry):
        at = pl.ds(pl.multiple_of(j * pair, pair), pair)
        outs = []
        for b in range(2):
            q = qbuf[b, :, at]
            zero = jnp.zeros_like(q)
            both = jnp.concatenate([jnp.where(first, q, zero), jnp.where(first, zero, q)], axis=0)
            scores = lax.dot_general(
                both, kbuf[b, :, at], (((1,), (1,)), ((), ())),
                preferred_element_type=jnp.float32,
            ) + bias
            top = jnp.max(scores, axis=-1, keepdims=True)
            expon = jnp.exp(scores - top)
            inv = 1.0 / jnp.sum(expon, axis=-1, keepdims=True)
            probs = (expon * inv).astype(jnp.bfloat16)
            att = jnp.dot(probs, vbuf[b, :, at], preferred_element_type=jnp.float32)
            att = jnp.where(first, att[:tokens], att[tokens:])
            outs.append(att.astype(jnp.bfloat16).astype(jnp.float32))
        mixture = outs[1] + guidance * (outs[0] - outs[1])
        upper = mixture.astype(jnp.bfloat16)
        mix_out[j, 0:tokens] = upper
        mix_out[j, tokens : 2 * tokens] = (mixture - upper.astype(jnp.float32)).astype(jnp.bfloat16)
        rolled(j).start()
        return carry

    lax.fori_loop(0, cols // pair, heads, 0)

    wo_copy.wait()
    tiles = half // OUT_TILE

    def partial(side, j):
        at = pl.ds(pl.multiple_of(side * half + j * OUT_TILE, OUT_TILE), OUT_TILE)
        res = jnp.dot(mix[...], wout[:, at], preferred_element_type=jnp.float32)
        return res[:tokens] + res[tokens:]

    def hand(j):
        return remote(give.at[j], take.at[j], give_send.at[j], take_recv.at[j], p, o)

    for j in range(cols // pair):
        rolled(j).wait_recv()
    coef_copy.wait_recv()
    for j in range(tiles):
        give[j] = partial(o, j)
        hand(j).start()
    keep = coefs[1, 0, 0:1, 0:1]
    noise = coefs[1, 1, 0:1, 0:1]
    before = low * X + (1 - low) * R
    for j in range(tiles):
        at = slice(j * OUT_TILE, (j + 1) * OUT_TILE)
        mine = partial(t, j)
        hand(j).wait_recv()
        guided = mine + take[j]
        current = frames[before, t, :, at].astype(jnp.float32)
        out_ref[:, at] = (keep * current - noise * guided).astype(out_ref.dtype)

    for c in range(CHUNKS):
        own_to(X, c).wait_send()
        own_to(Y, c).wait_send()
        for slot in (OWN, X, Y):
            to_partner(slot, c).wait_send()

        @pl.when(has_zto)
        def _(c=c):
            y_to_z(c).wait_send()

        @pl.when(has_zfrom)
        def _(c=c):
            to_partner(Z, c).wait_send()

        @pl.when(relays_y | (has_zfrom if c < SPLIT else has_zto))
        def _(c=c):
            slot_to_r(Y, c).wait_send()

        if c >= SPLIT:
            @pl.when(relays_z & has_zfrom)
            def _(c=c):
                x_to_far(c).wait_send()

        @pl.when(has_r)
        def _(c=c):
            to_partner(R, c).wait_send()
    for d in (1, -1, 2, -2):
        @pl.when((p + d >= 0) & (p + d < n))
        def _(d=d):
            mod_to(d).wait_send()
    for j in range(tiles):
        hand(j).wait_send()
    for j in range(cols // pair):
        rolled(j).wait_send()
    coef_copy.wait_send()

    @pl.when(p == n - 1)
    def _():
        wrap_copy.wait_send()


def on_device(
    latent, step_index, back_reach, ahead_reach, level_mod, text_mod,
    w_qkv, w_out, keep_coef, noise_coef,
):
    n = lax.axis_size("queue")
    _, tokens, half = latent.shape
    cols = w_qkv.shape[2]
    tiles = half // OUT_TILE
    pairs = cols // (2 * HDIM)
    dma = pltpu.SemaphoreType.DMA
    bf16, f32 = jnp.bfloat16, jnp.float32
    smem = pl.BlockSpec(memory_space=pltpu.SMEM)
    vmem = pl.BlockSpec(memory_space=pltpu.VMEM)
    hbm = pl.BlockSpec(memory_space=pl.ANY)
    out = pl.pallas_call(
        functools.partial(kernel, n),
        out_shape=jax.ShapeDtypeStruct((tokens, half), bf16),
        in_specs=[smem] * 5 + [vmem] * 2 + [hbm] * 3,
        out_specs=vmem,
        scratch_shapes=[
            pltpu.VMEM((SPAN, 2, tokens, half), bf16),
            pltpu.VMEM((SPAN, 2, 2 * half), f32),
            pltpu.VMEM(w_qkv.shape, bf16),
            pltpu.VMEM(w_out.shape, bf16),
            pltpu.VMEM((4 * tokens, 2 * half), bf16),
            pltpu.VMEM((2, tokens, cols), bf16),
            pltpu.VMEM((2, SPAN * tokens, cols), bf16),
            pltpu.VMEM((2, SPAN * tokens, cols), bf16),
            pltpu.VMEM((2 * tokens, cols), bf16),
            pltpu.VMEM((tiles, tokens, OUT_TILE), f32),
            pltpu.VMEM((tiles, tokens, OUT_TILE), f32),
            pltpu.VMEM((pairs, 2 * tokens, 2 * HDIM), bf16),
            pltpu.VMEM((2, 2, 8, 128), f32),
            pltpu.VMEM((tokens // 2, half), bf16),
            dma, dma((3,)), dma,
            dma((SPAN,)), dma((SPAN,)),
            dma((SPAN, CHUNKS)), dma((SPAN, CHUNKS)),
            dma((2, CHUNKS)), dma((CHUNKS,)), dma((CHUNKS,)), dma((4, CHUNKS)),
            dma((tiles,)), dma((tiles,)), dma((pairs,)), dma((pairs,)),
            dma, dma, dma, dma, dma((CHUNKS - SPLIT,)), dma((CHUNKS - SPLIT,)),
        ],
        compiler_params=pltpu.CompilerParams(
            collective_id=0, has_side_effects=True, vmem_limit_bytes=62 * 1024 * 1024
        ),
    )(
        step_index, back_reach, ahead_reach, keep_coef, noise_coef, level_mod, text_mod,
        latent, w_qkv, w_out,
    )
    return out[None]


def solution(mesh):
    return jax.shard_map(
        on_device,
        mesh=mesh,
        in_specs=(
            P("queue", None, "tp"),
            P("queue"),
            P("queue"),
            P("queue"),
            P(),
            P(),
            P(None, None, "tp"),
            P("tp", None),
            P(),
            P(),
        ),
        out_specs=P("queue", None, "tp"),
        check_vma=False,
    )
```
